128 devices in a mesh: wide: 16 (over y, x), narrow: 8 (over z, core).
Axes of the slice: x: 4, y: 4, z: 4, core: 2. Of those that a mesh axis runs over, the one named last changes fastest.
Arguments:
- old_fields: float32 [1024, 3, 32768], P(('wide', 'narrow')), may hold values from -6 to 6
- old_source: float32 [1024, 3, 32768], P(('wide', 'narrow')), may hold values from -12 to 12
- old_kappa: float32 [1024, 32768], P(('wide', 'narrow')), may hold values from 0.05 to 4
- patch_ids: int32 [1024], P(('wide', 'narrow')), may hold values from -1 to 511, as said below
Outputs:
- solution: float32 [3, 256, 512, 128], P(None, 'narrow', 'wide')
The draws below stay inside these ranges and needn't reach their ends.
Inputs may be any that keep to these rules, and one draw needn't show every extreme that they name: `patch_ids`: every patch number of 0 to 511 stands in exactly one slot, on a device with the same index of narrow as the device whose block of solution holds its box. From the slots of one device at most 2 patches go to the block of any one device, and exactly 2 to some device in every index of narrow. The block of every device receives exactly 4 patches. In every index of narrow some device has all its 8 slots filled and another none.
All inputs are finite; a program needn't handle non-finite values.
Results may differ from the reference program's by a relative error of at most 0.00002.
Values sent between devices are 32-bit elements; how exact they have to be, the bound alone decides.
A program may use at most 256 MiB of HBM per device.

```python
import math
import jax
import jax.numpy as jnp

PS = 32
BXR = 1
BYD = 1
BZ = 4
SWEEPS = 3
K = 4
CELLS = 32768
SLOTS = 8
LZ = 128
NX = 256
NY = 512
PATCHES = 512
N_WIDE = 16
N_NARROW = 8


def row_table(key, row_index):
    subkeys = jax.random.split(jax.random.fold_in(key, row_index), 6)
    columns = jnp.arange(N_WIDE, dtype=jnp.int32)
    code = jax.random.permutation(subkeys[0], N_WIDE).astype(jnp.int32)
    offset = jax.random.randint(subkeys[1], (), 0, N_WIDE).astype(jnp.int32)
    relative = (columns - offset) % N_WIDE
    pair_id = relative // 2
    first = relative % 2 == 0
    partner = jnp.where(first, (columns + 1) % N_WIDE, (columns - 1) % N_WIDE)
    flips = jax.random.randint(subkeys[2], (N_WIDE // 2,), 0, 2).astype(jnp.int32)
    amounts = jax.random.randint(subkeys[3], (N_WIDE // 2,), 0, K + 1).astype(jnp.int32)
    amounts = amounts.at[0].set(K)
    gain_first = flips[pair_id] == 1
    gainer = first == gain_first
    amount = amounts[pair_id]
    loser = jnp.where(gainer, partner, columns)
    base = ((code[None, :] - columns[:, None]) % N_WIDE < K).astype(jnp.int32)
    move = ((code[None, :] - loser[:, None]) % N_WIDE < amount[:, None]).astype(jnp.int32)
    matrix = base + jnp.where(gainer[:, None], move, -move)
    running = jnp.cumsum(matrix, axis=0)
    slot_range = jnp.arange(K, dtype=jnp.int32)
    labels = jnp.sum((running[:, :, None] <= slot_range[None, None, :]).astype(jnp.int32), axis=0)
    shuffles = jax.vmap(lambda sub: jax.random.permutation(sub, K))(jax.random.split(subkeys[4], N_WIDE))
    shuffled = jnp.take_along_axis(labels, shuffles, axis=1)
    flat_src = shuffled.reshape(N_WIDE * K)
    visit_order = jax.random.permutation(subkeys[5], N_WIDE * K)
    visited = flat_src[visit_order]
    onehot = (visited[:, None] == columns[None, :]).astype(jnp.int32)
    before = jnp.cumsum(onehot, axis=0) - onehot
    rank_visit = jnp.sum(before * onehot, axis=1)
    rank_flat = jnp.zeros((N_WIDE * K,), jnp.int32).at[visit_order].set(rank_visit)
    flat_index = jnp.arange(N_WIDE * K, dtype=jnp.int32)
    owner = flat_index // K
    local_slot = flat_index % K
    part_x = local_slot // (BYD * BZ)
    part_y = local_slot // BZ % BYD
    part_z = local_slot % BZ
    box_x = row_index * BXR + part_x
    box_y = owner * BYD + part_y
    identities = (box_x * (N_WIDE * BYD) + box_y) * BZ + part_z
    slot_table = jnp.full((N_WIDE, SLOTS), -1, jnp.int32).at[flat_src, rank_flat].set(identities)
    return slot_table


def draw_patch_ids(key, part):
    tables = jnp.stack([row_table(key, row_index) for row_index in range(N_NARROW)])
    return tables.transpose(1, 0, 2).reshape(N_WIDE * N_NARROW * SLOTS)


def shard_levels(key, shape, cuts, low, top_value):
    def one(dim, blocks):
        steps = jax.random.uniform(jax.random.fold_in(jax.random.fold_in(key, 6), dim), (blocks,), jnp.float32, low / len(cuts), top_value / len(cuts))
        return jnp.repeat(jnp.exp(steps), shape[dim] // blocks).reshape((-1,) + (1,) * (len(shape) - dim - 1))

    level = one(*cuts[0])
    for cut in cuts[1:]:
        level = level * one(*cut)
    return level


def normal_values(own_key, shape, scale, reach, shards=(), kind=jnp.bfloat16):
    gain = shard_levels(own_key, shape, shards, -0.22, 0.18) if shards else 1.0
    array = jax.random.normal(own_key, shape, jnp.float32) * scale * gain
    return jnp.minimum(jnp.maximum(array, -reach), reach).astype(kind)


def setup_inputs(seed: int = 0) -> dict:
    arg_keys = jax.random.split(jax.random.key(seed), 5)
    return {
        "old_fields": normal_values(arg_keys[0], (N_WIDE * N_NARROW * SLOTS, 3, CELLS), 1.0, 6.0, ((0, 128),), jnp.float32),
        "old_source": normal_values(arg_keys[1], (N_WIDE * N_NARROW * SLOTS, 3, CELLS), 2.0, 12.0, ((0, 128),), jnp.float32),
        "old_kappa": jnp.clip(jnp.exp(math.log(4.0) - 4.3820266 * jax.random.uniform(arg_keys[2], (N_WIDE * N_NARROW * SLOTS, CELLS), jnp.float32) ** shard_levels(arg_keys[2], (N_WIDE * N_NARROW * SLOTS, CELLS), ((0, 128),), -0.2, 0.2)), 0.05, 4.0),
        "patch_ids": draw_patch_ids(jax.random.fold_in(arg_keys[4], 71), 0),
    }


OMEGA = 1.5


def six_sum(values):
    widths = [(0, 0)] * (values.ndim - 3) + [(1, 1)] * 3
    padded = jnp.pad(values, widths)
    return (padded[..., 2:, 1:-1, 1:-1] + padded[..., :-2, 1:-1, 1:-1]
            + padded[..., 1:-1, 2:, 1:-1] + padded[..., 1:-1, :-2, 1:-1]
            + padded[..., 1:-1, 1:-1, 2:] + padded[..., 1:-1, 1:-1, :-2])


def reference(old_fields, old_source, old_kappa, patch_ids):
    payload = jnp.concatenate([old_fields, old_source, old_kappa[:, None, :]], axis=1)
    targets = jnp.where(patch_ids >= 0, patch_ids, PATCHES).astype(jnp.int32)
    patches = jnp.zeros((PATCHES, 7, CELLS), jnp.float32).at[targets].set(payload, mode="drop")
    blocks = patches.reshape(N_NARROW * BXR, N_WIDE * BYD, BZ, 7, PS, PS, PS)
    blocks = blocks.transpose(3, 0, 4, 1, 5, 2, 6).reshape(7, NX, NY, LZ)
    current = blocks[0:3]
    source = blocks[3:6]
    inverse = 1.0 / (6.0 + blocks[6])
    coord_x = jnp.arange(NX, dtype=jnp.int32)[:, None, None]
    coord_y = jnp.arange(NY, dtype=jnp.int32)[None, :, None]
    coord_z = jnp.arange(LZ, dtype=jnp.int32)[None, None, :]
    parity = (coord_x + coord_y + coord_z) % 2
    for sweep_number in range(SWEEPS):
        for colour in (0, 1):
            update = current + OMEGA * ((source + six_sum(current)) * inverse - current)
            current = jnp.where(parity == colour, update, current)
    return current
```

```python
import jax
import jax.numpy as jnp
from jax import lax
from jax.experimental import pallas as pl
from jax.experimental.pallas import tpu as pltpu
from jax.sharding import PartitionSpec as P

PS = 32
SLOTS = 8
LANES = 128
WIDE = 16
STAGES = 7
CHUNK = 128
PIECE = 64
HALF_SWEEPS = 6
FACE = 96
MESH = pl.DeviceIdType.MESH
F32 = jnp.float32


def row_peer(me, offset):
    row = lax.rem(me // 4 + offset // 4, 4)
    column = lax.rem(lax.rem(me, 4) + lax.rem(offset, 4), 4)
    return row * 4 + column


def kernel(fields, source, kappa, labels, out, *scratch):
    received = scratch[0:STAGES]
    sending = scratch[STAGES : 2 * STAGES]
    (
        cells, rhs, weight, all_labels, start_vmem, start_smem, faces_out, faces_in,
        label_send, label_recv, spread_send, spread_recv, give_send, give_recv,
        own_spread, own_give, start_sem, face_send, face_recv,
    ) = scratch[2 * STAGES :]
    me = lax.axis_index("wide")
    level = lax.axis_index("narrow")
    levels = lax.axis_size("narrow")
    below, above = level > 0, level < levels - 1
    left, right = me > 0, me < WIDE - 1

    faces_in[...] = jnp.zeros_like(faces_in)

    barrier = pltpu.get_barrier_semaphore()

    def greet(offset, carry):
        pl.semaphore_signal(
            barrier, inc=1, device_id=(row_peer(me, offset), level), device_id_type=MESH
        )
        return carry

    lax.fori_loop(1, WIDE, greet, 0)

    @pl.when(below)
    def _():
        pl.semaphore_signal(barrier, inc=1, device_id=(me, level - 1), device_id_type=MESH)

    @pl.when(above)
    def _():
        pl.semaphore_signal(barrier, inc=1, device_id=(me, level + 1), device_id_type=MESH)

    pl.semaphore_wait(
        barrier, WIDE - 1 + below.astype(jnp.int32) + above.astype(jnp.int32)
    )

    def label_copy(target, origin):
        return pltpu.make_async_remote_copy(
            src_ref=labels,
            dst_ref=all_labels.at[pl.ds(origin * SLOTS, SLOTS), :],
            send_sem=label_send.at[target],
            recv_sem=label_recv.at[origin],
            device_id=(target, level),
            device_id_type=MESH,
        )

    def send_label(offset, carry):
        label_copy(row_peer(me, offset), me).start()
        return carry

    lax.fori_loop(1, WIDE, send_label, 0)
    all_labels[pl.ds(me * SLOTS, SLOTS), :] = labels[...]

    def slots_of(stage, part):
        rows = pl.ds(part * CHUNK, CHUNK)
        if stage == 0:
            return kappa.at[rows, :]
        if stage < 4:
            return fields.at[stage - 1, rows, :]
        return source.at[stage - 4, rows, :]

    def spread_copy(stage, target, origin):
        return pltpu.make_async_remote_copy(
            src_ref=slots_of(stage, target),
            dst_ref=received[stage].at[pl.ds(origin * CHUNK, CHUNK), :],
            send_sem=spread_send.at[stage, target],
            recv_sem=spread_recv.at[stage, origin],
            device_id=(target, level),
            device_id_type=MESH,
        )

    def own_spread_copy(stage):
        return pltpu.make_async_copy(
            slots_of(stage, me),
            received[stage].at[pl.ds(me * CHUNK, CHUNK), :],
            own_spread.at[stage],
        )

    for stage in range(STAGES):

        def send_spread(offset, carry):
            spread_copy(stage, row_peer(me, offset), me).start()
            return carry

        lax.fori_loop(1, WIDE, send_spread, 0)
        own_spread_copy(stage).start()

    def wait_label(offset, carry):
        origin = row_peer(me, offset)
        label_copy(origin, origin).wait_recv()
        return carry

    lax.fori_loop(1, WIDE, wait_label, 0)
    slot_row = lax.broadcasted_iota(jnp.int32, (WIDE * SLOTS, LANES), 0)
    wanted = lax.broadcasted_iota(jnp.int32, (WIDE * SLOTS, LANES), 1) + level * (WIDE * 4)
    first = (slot_row // SLOTS) * CHUNK + slot_row % SLOTS
    found = jnp.where(all_labels[...] == wanted, first, 0)
    start_vmem[...] = jnp.max(found, axis=0, keepdims=True)
    move = pltpu.make_async_copy(start_vmem, start_smem, start_sem)
    move.start()
    move.wait()

    lane = lax.broadcasted_iota(jnp.int32, (8, LANES), 1)
    low_half = lane < 64
    low_quarter = lane % 64 < 32

    def place_of(stage, origin):
        if stage == 0:
            return weight.at[pl.ds(origin * PIECE, PIECE), :]
        base = ((stage - 1) % 3) * PS * PS
        home = cells if stage < 4 else rhs
        return home.at[pl.ds(base + origin * PIECE, PIECE), :]

    def give_copy(stage, target, origin):
        return pltpu.make_async_remote_copy(
            src_ref=sending[stage].at[pl.ds(target * PIECE, PIECE), :],
            dst_ref=place_of(stage, origin),
            send_sem=give_send.at[stage, target],
            recv_sem=give_recv.at[stage, origin],
            device_id=(target, level),
            device_id_type=MESH,
        )

    def own_give_copy(stage):
        return pltpu.make_async_copy(
            sending[stage].at[pl.ds(me * PIECE, PIECE), :],
            place_of(stage, me),
            own_give.at[stage],
        )

    for stage in range(STAGES):

        def wait_spread(offset, carry):
            origin = row_peer(me, offset)
            spread_copy(stage, origin, origin).wait_recv()
            return carry

        lax.fori_loop(1, WIDE, wait_spread, 0)
        own_spread_copy(stage).wait()

        def pick(owner, carry):
            starts = [start_smem[0, owner * 4 + part] for part in range(4)]
            for plane in range(2):
                v = [
                    received[stage][pl.ds(start + plane * 64, 8, stride=8), :]
                    for start in starts
                ]
                u = [
                    jnp.where(low_half, v[0], pltpu.roll(v[2], 64, 1)),
                    jnp.where(low_half, v[1], pltpu.roll(v[3], 64, 1)),
                    jnp.where(low_half, pltpu.roll(v[0], 64, 1), v[2]),
                    jnp.where(low_half, pltpu.roll(v[1], 64, 1), v[3]),
                ]
                w = [
                    jnp.where(low_quarter, u[0], pltpu.roll(u[1], 32, 1)),
                    jnp.where(low_quarter, pltpu.roll(u[0], 96, 1), u[1]),
                    jnp.where(low_quarter, u[2], pltpu.roll(u[3], 32, 1)),
                    jnp.where(low_quarter, pltpu.roll(u[2], 96, 1), u[3]),
                ]
                for part in range(4):
                    row = owner * PIECE + plane * PS + part
                    sending[stage][pl.ds(row, 8, stride=4), :] = w[part]
            return carry

        lax.fori_loop(0, WIDE, pick, 0)

        def send_give(offset, carry):
            give_copy(stage, row_peer(me, offset), me).start()
            return carry

        lax.fori_loop(1, WIDE, send_give, 0)
        own_give_copy(stage).start()

    for stage in range(STAGES):

        def wait_give(offset, carry):
            origin = row_peer(me, offset)
            give_copy(stage, origin, origin).wait_recv()
            return carry

        lax.fori_loop(1, WIDE, wait_give, 0)
        own_give_copy(stage).wait()
        if stage == 0:

            def invert(block, carry):
                rows = pl.ds(pl.multiple_of(block * PS, PS), PS)
                weight[rows, :] = 1.5 * (1.0 / (6.0 + weight[rows, :]))
                return carry

            lax.fori_loop(0, PS, invert, 0)

    ways = (
        (above, (me, level + 1), below),
        (below, (me, level - 1), above),
        (right, (me + 1, level), left),
        (left, (me - 1, level), right),
    )

    def face_copy(slot, way):
        return pltpu.make_async_remote_copy(
            src_ref=faces_out.at[slot, way],
            dst_ref=faces_in.at[slot, way],
            send_sem=face_send.at[slot, way],
            recv_sem=face_recv.at[slot, way],
            device_id=ways[way][1],
            device_id_type=MESH,
        )

    row32 = lax.broadcasted_iota(jnp.int32, (PS, LANES), 0)
    lane32 = lax.broadcasted_iota(jnp.int32, (PS, LANES), 1)
    odd = (row32 + lane32) % 2
    first_row, last_row = row32 == 0, row32 == PS - 1
    first_lane, last_lane = lane32 == 0, lane32 == LANES - 1

    for step in range(HALF_SWEEPS):
        slot, colour = step % 2, step % 2
        if step >= 2:
            for way in range(4):

                @pl.when(ways[way][0])
                def _():
                    face_copy(slot, way).wait_send()

        for field in range(3):
            base = field * PS * PS
            faces_out[slot, 0, pl.ds(field * PS, PS), :] = cells[pl.ds(base + (PS - 1) * PS, PS), :]
            faces_out[slot, 1, pl.ds(field * PS, PS), :] = cells[pl.ds(base, PS), :]
        for group in range(FACE // 8):
            rows = pl.ds(group * 8, 8)
            faces_out[slot, 2, rows, :] = cells[pl.ds(group * 8 * PS + PS - 1, 8, stride=PS), :]
            faces_out[slot, 3, rows, :] = cells[pl.ds(group * 8 * PS, 8, stride=PS), :]
        for way in range(4):

            @pl.when(ways[way][0])
            def _():
                face_copy(slot, way).start()

        for way in range(4):

            @pl.when(ways[way][2])
            def _():
                face_copy(slot, way).wait_recv()

        def relax(plane, before_of, after_of):
            mine = (odd + plane) % 2 == colour
            w = weight[pl.ds(pl.multiple_of(plane * PS, PS), PS), :]
            for field in range(3):
                base = pl.multiple_of(field * PS * PS + plane * PS, PS)
                v = cells[pl.ds(base, PS), :]
                line = field * PS + plane
                low = jnp.broadcast_to(faces_in[slot, 2, pl.ds(line, 1), :], (PS, LANES))
                high = jnp.broadcast_to(faces_in[slot, 3, pl.ds(line, 1), :], (PS, LANES))
                total = before_of(field, base) + after_of(field, base)
                total += jnp.where(first_row, low, pltpu.roll(v, 1, 0))
                total += jnp.where(last_row, high, pltpu.roll(v, PS - 1, 0))
                total += jnp.where(first_lane, 0.0, pltpu.roll(v, 1, 1))
                total += jnp.where(last_lane, 0.0, pltpu.roll(v, LANES - 1, 1))
                fresh = (rhs[pl.ds(base, PS), :] + total) * w - 0.5 * v
                fresh = jnp.where(mine, fresh, v)
                if step == HALF_SWEEPS - 1:
                    out[field, plane] = fresh
                else:
                    cells[pl.ds(base, PS), :] = fresh

        def below_face(field, base):
            return faces_in[slot, 0, pl.ds(field * PS, PS), :]

        def above_face(field, base):
            return faces_in[slot, 1, pl.ds(field * PS, PS), :]

        def before(field, base):
            return cells[pl.ds(pl.multiple_of(base - PS, PS), PS), :]

        def after(field, base):
            return cells[pl.ds(pl.multiple_of(base + PS, PS), PS), :]

        relax(0, below_face, after)

        def inner(plane, carry):
            relax(plane, before, after)
            return carry

        lax.fori_loop(1, PS - 1, inner, 0)
        relax(PS - 1, before, above_face)

    for slot in range(2):
        for way in range(4):

            @pl.when(ways[way][0])
            def _():
                face_copy(slot, way).wait_send()

    def drain(offset, carry):
        target = row_peer(me, offset)
        label_copy(target, me).wait_send()
        for stage in range(STAGES):
            spread_copy(stage, target, me).wait_send()
            give_copy(stage, target, me).wait_send()
        return carry

    lax.fori_loop(1, WIDE, drain, 0)


def local(old_fields, old_source, old_kappa, patch_ids):
    def tiles(array):
        lead = array.shape[:-2]
        split = array.reshape(lead + (SLOTS, -1, LANES))
        return jnp.swapaxes(split, -3, -2).reshape(lead + (-1, LANES))

    fields = tiles(jnp.swapaxes(old_fields, 0, 1))
    source = tiles(jnp.swapaxes(old_source, 0, 1))
    kappa = tiles(old_kappa)
    labels = jnp.broadcast_to(patch_ids[:, None], (SLOTS, LANES))
    vmem = pl.BlockSpec(memory_space=pltpu.VMEM)
    anywhere = pl.BlockSpec(memory_space=pl.ANY)
    dma = pltpu.SemaphoreType.DMA
    scratch = (
        [pltpu.VMEM((WIDE * CHUNK, LANES), F32)] * STAGES
        + [pltpu.VMEM((WIDE * PIECE, LANES), F32)] * STAGES
        + [
            pltpu.VMEM((3 * PS * PS, LANES), F32),
            pltpu.VMEM((3 * PS * PS, LANES), F32),
            pltpu.VMEM((PS * PS, LANES), F32),
            pltpu.VMEM((WIDE * SLOTS, LANES), jnp.int32),
            pltpu.VMEM((1, LANES), jnp.int32),
            pltpu.SMEM((1, LANES), jnp.int32),
            pltpu.VMEM((2, 4, FACE, LANES), F32),
            pltpu.VMEM((2, 4, FACE, LANES), F32),
            dma((WIDE,)),
            dma((WIDE,)),
            dma((STAGES, WIDE)),
            dma((STAGES, WIDE)),
            dma((STAGES, WIDE)),
            dma((STAGES, WIDE)),
            dma((STAGES,)),
            dma((STAGES,)),
            dma(()),
            dma((2, 4)),
            dma((2, 4)),
        ]
    )
    return pl.pallas_call(
        kernel,
        out_shape=jax.ShapeDtypeStruct((3, PS, PS, LANES), F32),
        in_specs=[anywhere, anywhere, anywhere, vmem],
        out_specs=vmem,
        scratch_shapes=scratch,
        compiler_params=pltpu.CompilerParams(
            collective_id=0, has_side_effects=True, vmem_limit_bytes=60 << 20
        ),
        name="regrid_and_sweep",
    )(fields, source, kappa, labels)


def solution(mesh):
    in_specs = (
        P(("wide", "narrow"), None, None),
        P(("wide", "narrow"), None, None),
        P(("wide", "narrow"), None),
        P(("wide", "narrow")),
    )
    out_specs = P(None, "narrow", "wide", None)
    return jax.shard_map(local, mesh=mesh, in_specs=in_specs, out_specs=out_specs, check_vma=False)
```

```python
import jax
import jax.numpy as jnp
from jax import lax
from jax.experimental import pallas as pl
from jax.experimental.pallas import tpu as pltpu
from jax.sharding import PartitionSpec as P

PS = 32
SLOTS = 8
LANES = 128
WIDE = 16
STAGES = 7
CHUNK = 128
PIECE = 64
HALF_SWEEPS = 6
GROUP = 4
MESH = pl.DeviceIdType.MESH
F32 = jnp.float32


def row_peer(me, offset):
    row = lax.rem(me // 4 + offset // 4, 4)
    column = lax.rem(lax.rem(me, 4) + lax.rem(offset, 4), 4)
    return row * 4 + column


def kernel(fields, source, kappa, labels, out, *scratch):
    received = scratch[0:STAGES]
    sending = scratch[STAGES : 2 * STAGES]
    cells = scratch[2 * STAGES : 2 * STAGES + 3]
    rhs = scratch[2 * STAGES + 3 : 2 * STAGES + 6]
    (
        weight, all_labels, start_vmem, start_smem, faces_out, faces_in,
        label_send, label_recv, spread_send, spread_recv, give_send, give_recv,
        own_spread, own_give, start_sem, face_send, face_recv,
    ) = scratch[2 * STAGES + 6 :]
    me = lax.axis_index("wide")
    level = lax.axis_index("narrow")
    levels = lax.axis_size("narrow")
    below, above = level > 0, level < levels - 1
    left, right = me > 0, me < WIDE - 1

    faces_in[...] = jnp.zeros_like(faces_in)

    barrier = pltpu.get_barrier_semaphore()

    def greet(offset, carry):
        pl.semaphore_signal(
            barrier, inc=1, device_id=(row_peer(me, offset), level), device_id_type=MESH
        )
        return carry

    lax.fori_loop(1, WIDE, greet, 0)

    @pl.when(below)
    def _():
        pl.semaphore_signal(barrier, inc=1, device_id=(me, level - 1), device_id_type=MESH)

    @pl.when(above)
    def _():
        pl.semaphore_signal(barrier, inc=1, device_id=(me, level + 1), device_id_type=MESH)

    pl.semaphore_wait(
        barrier, WIDE - 1 + below.astype(jnp.int32) + above.astype(jnp.int32)
    )

    def label_copy(target, origin):
        return pltpu.make_async_remote_copy(
            src_ref=labels,
            dst_ref=all_labels.at[pl.ds(origin * SLOTS, SLOTS), :],
            send_sem=label_send.at[target],
            recv_sem=label_recv.at[origin],
            device_id=(target, level),
            device_id_type=MESH,
        )

    def send_label(offset, carry):
        label_copy(row_peer(me, offset), me).start()
        return carry

    def slots_of(stage, part):
        rows = pl.ds(part * CHUNK, CHUNK)
        if stage == 0:
            return kappa.at[rows, :]
        return (source if stage % 2 == 0 else fields).at[(stage - 1) // 2, rows, :]

    def spread_copy(stage, target, origin):
        return pltpu.make_async_remote_copy(
            src_ref=slots_of(stage, target),
            dst_ref=received[stage].at[pl.ds(origin * CHUNK, CHUNK), :],
            send_sem=spread_send.at[stage, target],
            recv_sem=spread_recv.at[stage, origin],
            device_id=(target, level),
            device_id_type=MESH,
        )

    def own_spread_copy(stage):
        return pltpu.make_async_copy(
            slots_of(stage, me),
            received[stage].at[pl.ds(me * CHUNK, CHUNK), :],
            own_spread.at[stage],
        )

    def spread(stage, first, last):
        def send_spread(turn, carry):
            spread_copy(stage, row_peer(me, (turn * 7) % WIDE), me).start()
            return carry

        lax.fori_loop(first, last, send_spread, 0)
        if first == 1:
            own_spread_copy(stage).start()

    def place_of(stage, origin):
        if stage == 0:
            return weight.at[pl.ds(origin * PIECE, PIECE), :]
        if stage % 2 == 0:
            return rhs[(stage - 1) // 2].at[pl.ds(origin * PIECE, PIECE), :]
        return cells[(stage - 1) // 2].at[pl.ds(origin * PIECE + PS, PIECE), :]

    def give_copy(stage, target, origin):
        return pltpu.make_async_remote_copy(
            src_ref=sending[stage].at[pl.ds(target * PIECE, PIECE), :],
            dst_ref=place_of(stage, origin),
            send_sem=give_send.at[stage, target],
            recv_sem=give_recv.at[stage, origin],
            device_id=(target, level),
            device_id_type=MESH,
        )

    def own_give_copy(stage):
        return pltpu.make_async_copy(
            sending[stage].at[pl.ds(me * PIECE, PIECE), :],
            place_of(stage, me),
            own_give.at[stage],
        )

    lane = lax.broadcasted_iota(jnp.int32, (8, LANES), 1)
    low_half = lane < 64
    low_quarter = lane % 64 < 32

    def give(stage):
        def wait_spread(turn, carry):
            origin = row_peer(me, turn)
            spread_copy(stage, origin, origin).wait_recv()
            return carry

        lax.fori_loop(1, WIDE, wait_spread, 0)
        own_spread_copy(stage).wait()

        def pick(owner, carry):
            starts = [start_smem[0, owner * 4 + part] for part in range(4)]
            v = [
                [
                    received[stage][pl.ds(start + plane * 64, 8, stride=8), :]
                    for start in starts
                ]
                for plane in range(2)
            ]
            for plane in range(2):
                a, b, c, d = v[plane]
                u = [
                    jnp.where(low_half, a, pltpu.roll(c, 64, 1)),
                    jnp.where(low_half, b, pltpu.roll(d, 64, 1)),
                    jnp.where(low_half, pltpu.roll(a, 64, 1), c),
                    jnp.where(low_half, pltpu.roll(b, 64, 1), d),
                ]
                w = [
                    jnp.where(low_quarter, u[0], pltpu.roll(u[1], 32, 1)),
                    jnp.where(low_quarter, pltpu.roll(u[0], 96, 1), u[1]),
                    jnp.where(low_quarter, u[2], pltpu.roll(u[3], 32, 1)),
                    jnp.where(low_quarter, pltpu.roll(u[2], 96, 1), u[3]),
                ]
                for part in range(4):
                    row = owner * PIECE + plane * PS + part
                    sending[stage][pl.ds(row, 8, stride=4), :] = w[part]
            return carry

        lax.fori_loop(0, WIDE, pick, 0)

        def send_give(turn, carry):
            give_copy(stage, row_peer(me, (turn * 7) % WIDE), me).start()
            return carry

        lax.fori_loop(1, WIDE, send_give, 0)
        own_give_copy(stage).start()

    def wait_given(stage):
        def wait_give(turn, carry):
            origin = row_peer(me, turn)
            give_copy(stage, origin, origin).wait_recv()
            return carry

        lax.fori_loop(1, WIDE, wait_give, 0)
        own_give_copy(stage).wait()

    ways = (
        (above, (me, level + 1), below),
        (below, (me, level - 1), above),
        (right, (me + 1, level), left),
        (left, (me - 1, level), right),
    )

    def face_copy(field, slot, way):
        return pltpu.make_async_remote_copy(
            src_ref=faces_out.at[field, slot, way],
            dst_ref=faces_in.at[field, slot, way],
            send_sem=face_send.at[field, slot, way],
            recv_sem=face_recv.at[field, slot, way],
            device_id=ways[way][1],
            device_id_type=MESH,
        )

    def face_sent(field, step):
        for way in range(4):

            @pl.when(ways[way][0])
            def _():
                face_copy(field, step % 2, way).wait_send()

    def post(field, step):
        slot = step % 2
        if step >= 2:
            face_sent(field, step - 2)
        block = cells[field]
        faces_out[field, slot, 0] = block[PS * PS : (PS + 1) * PS, :]
        faces_out[field, slot, 1] = block[PS : 2 * PS, :]
        for group in range(PS // 8):
            rows, row = pl.ds(group * 8, 8), (group * 8 + 1) * PS
            faces_out[field, slot, 2, rows, :] = block[pl.ds(row + PS - 1, 8, stride=PS), :]
            faces_out[field, slot, 3, rows, :] = block[pl.ds(row, 8, stride=PS), :]
        for way in (2, 3, 0, 1):

            @pl.when(ways[way][0])
            def _():
                face_copy(field, slot, way).start()

    row32 = lax.broadcasted_iota(jnp.int32, (PS, LANES), 0)
    lane32 = lax.broadcasted_iota(jnp.int32, (PS, LANES), 1)
    even = (row32 + lane32) % 2 == 0
    odd = (row32 + lane32) % 2 == 1
    first_row, last_row = row32 == 0, row32 == PS - 1
    first_lane, last_lane = lane32 == 0, lane32 == LANES - 1

    def relax(field, step):
        slot, colour = step % 2, step % 2
        for way in range(4):

            @pl.when(ways[way][2])
            def _():
                face_copy(field, slot, way).wait_recv()

        block, right_side = cells[field], rhs[field]
        block[0:PS, :] = faces_in[field, slot, 0]
        block[(PS + 1) * PS : (PS + 2) * PS, :] = faces_in[field, slot, 1]

        def several(group, carry):
            plane = group * GROUP
            v = [
                block[pl.ds(pl.multiple_of((plane + i) * PS, PS), PS), :]
                for i in range(GROUP + 2)
            ]
            fresh = []
            for i in range(GROUP):
                rows = pl.ds(pl.multiple_of((plane + i) * PS, PS), PS)
                mine = v[i + 1]
                low = jnp.broadcast_to(
                    faces_in[field, slot, 2, pl.ds(plane + i, 1), :], (PS, LANES)
                )
                high = jnp.broadcast_to(
                    faces_in[field, slot, 3, pl.ds(plane + i, 1), :], (PS, LANES)
                )
                total = v[i] + v[i + 2]
                total += jnp.where(first_row, low, pltpu.roll(mine, 1, 0))
                total += jnp.where(last_row, high, pltpu.roll(mine, PS - 1, 0))
                total += jnp.where(first_lane, 0.0, pltpu.roll(mine, 1, 1))
                total += jnp.where(last_lane, 0.0, pltpu.roll(mine, LANES - 1, 1))
                value = (right_side[rows, :] + total) * weight[rows, :] - 0.5 * mine
                fresh.append(jnp.where(even if i % 2 == colour else odd, value, mine))
            for i in range(GROUP):
                if step == HALF_SWEEPS - 1:
                    out[field, plane + i] = fresh[i]
                else:
                    rows = pl.ds(pl.multiple_of((plane + i + 1) * PS, PS), PS)
                    block[rows, :] = fresh[i]
            return carry

        lax.fori_loop(0, PS // GROUP, several, 0)

    lax.fori_loop(1, WIDE, send_label, 0)
    all_labels[pl.ds(me * SLOTS, SLOTS), :] = labels[...]
    for stage in range(4):
        spread(stage, 1, WIDE)

    def wait_label(offset, carry):
        origin = row_peer(me, offset)
        label_copy(origin, origin).wait_recv()
        return carry

    lax.fori_loop(1, WIDE, wait_label, 0)
    slot_row = lax.broadcasted_iota(jnp.int32, (WIDE * SLOTS, LANES), 0)
    wanted = lax.broadcasted_iota(jnp.int32, (WIDE * SLOTS, LANES), 1) + level * (WIDE * 4)
    first = (slot_row // SLOTS) * CHUNK + slot_row % SLOTS
    found = jnp.where(all_labels[...] == wanted, first, 0)
    start_vmem[...] = jnp.max(found, axis=0, keepdims=True)
    move = pltpu.make_async_copy(start_vmem, start_smem, start_sem)
    move.start()
    move.wait()

    half = WIDE // 2
    for stage in range(3):
        give(stage)
    spread(4, 1, half)
    wait_given(0)

    def invert(block, carry):
        rows = pl.ds(pl.multiple_of(block * PS, PS), PS)
        weight[rows, :] = 1.5 * (1.0 / (6.0 + weight[rows, :]))
        return carry

    lax.fori_loop(0, PS, invert, 0)
    wait_given(1)
    wait_given(2)

    between = {
        (0, 0): lambda: spread(4, half, WIDE),
        (0, 1): lambda: give(3),
        (0, 2): lambda: spread(5, 1, half),
        (0, 3): lambda: spread(5, half, WIDE),
        (0, 4): lambda: give(4),
        (0, 5): lambda: spread(6, 1, half),
        (1, 0): lambda: spread(6, half, WIDE),
        (1, 1): lambda: give(5),
        (1, 3): lambda: give(6),
    }
    for field in range(3):
        if field > 0:
            wait_given(2 * field + 1)
            wait_given(2 * field + 2)
        for step in range(HALF_SWEEPS):
            post(field, step)
            if (field, step) in between:
                between[field, step]()
            relax(field, step)

    for field in range(3):
        face_sent(field, HALF_SWEEPS - 2)
        face_sent(field, HALF_SWEEPS - 1)

    def drain(offset, carry):
        target = row_peer(me, offset)
        label_copy(target, me).wait_send()
        for stage in range(STAGES):
            spread_copy(stage, target, me).wait_send()
            give_copy(stage, target, me).wait_send()
        return carry

    lax.fori_loop(1, WIDE, drain, 0)


def local(old_fields, old_source, old_kappa, patch_ids):
    def tiles(array):
        lead = array.shape[:-2]
        split = array.reshape(lead + (SLOTS, -1, LANES))
        return jnp.swapaxes(split, -3, -2).reshape(lead + (-1, LANES))

    fields = tiles(jnp.swapaxes(old_fields, 0, 1))
    source = tiles(jnp.swapaxes(old_source, 0, 1))
    kappa = tiles(old_kappa)
    labels = jnp.broadcast_to(patch_ids[:, None], (SLOTS, LANES))
    vmem = pl.BlockSpec(memory_space=pltpu.VMEM)
    anywhere = pl.BlockSpec(memory_space=pl.ANY)
    dma = pltpu.SemaphoreType.DMA
    scratch = (
        [pltpu.VMEM((WIDE * CHUNK, LANES), F32)] * STAGES
        + [pltpu.VMEM((WIDE * PIECE, LANES), F32)] * STAGES
        + [pltpu.VMEM(((PS + 2) * PS, LANES), F32)] * 3
        + [pltpu.VMEM((PS * PS, LANES), F32)] * 3
        + [
            pltpu.VMEM((PS * PS, LANES), F32),
            pltpu.VMEM((WIDE * SLOTS, LANES), jnp.int32),
            pltpu.VMEM((1, LANES), jnp.int32),
            pltpu.SMEM((1, LANES), jnp.int32),
            pltpu.VMEM((3, 2, 4, PS, LANES), F32),
            pltpu.VMEM((3, 2, 4, PS, LANES), F32),
            dma((WIDE,)),
            dma((WIDE,)),
            dma((STAGES, WIDE)),
            dma((STAGES, WIDE)),
            dma((STAGES, WIDE)),
            dma((STAGES, WIDE)),
            dma((STAGES,)),
            dma((STAGES,)),
            dma(()),
            dma((3, 2, 4)),
            dma((3, 2, 4)),
        ]
    )
    return pl.pallas_call(
        kernel,
        out_shape=jax.ShapeDtypeStruct((3, PS, PS, LANES), F32),
        in_specs=[anywhere, anywhere, anywhere, vmem],
        out_specs=vmem,
        scratch_shapes=scratch,
        compiler_params=pltpu.CompilerParams(
            collective_id=0, has_side_effects=True, vmem_limit_bytes=60 << 20
        ),
        name="regrid_and_sweep",
    )(fields, source, kappa, labels)


def solution(mesh):
    in_specs = (
        P(("wide", "narrow"), None, None),
        P(("wide", "narrow"), None, None),
        P(("wide", "narrow"), None),
        P(("wide", "narrow")),
    )
    out_specs = P(None, "narrow", "wide", None)
    return jax.shard_map(local, mesh=mesh, in_specs=in_specs, out_specs=out_specs, check_vma=False)
```

```python
import jax
import jax.numpy as jnp
from jax import lax
from jax.experimental import pallas as pl
from jax.experimental.pallas import tpu as pltpu
from jax.sharding import PartitionSpec as P

PS = 32
SLOTS = 8
LANES = 128
WIDE = 16
STAGES = 7
CHUNK = 128
PIECE = 64
HALF_SWEEPS = 6
GROUP = 4
MESH = pl.DeviceIdType.MESH
F32 = jnp.float32


def row_peer(me, offset):
    row = lax.rem(me // 4 + offset // 4, 4)
    column = lax.rem(lax.rem(me, 4) + lax.rem(offset, 4), 4)
    return row * 4 + column


def kernel(fields, source, kappa, labels, out, *scratch):
    received = scratch[0:STAGES]
    sending = scratch[STAGES : 2 * STAGES]
    cells = scratch[2 * STAGES : 2 * STAGES + 3]
    rhs = scratch[2 * STAGES + 3 : 2 * STAGES + 6]
    (
        weight, all_labels, start_vmem, start_smem, faces_out, faces_in,
        label_send, label_recv, spread_send, spread_recv, give_send, give_recv,
        own_spread, own_give, start_sem, face_send, face_recv,
    ) = scratch[2 * STAGES + 6 :]
    me = lax.axis_index("wide")
    level = lax.axis_index("narrow")
    levels = lax.axis_size("narrow")
    below, above = level > 0, level < levels - 1
    left, right = me > 0, me < WIDE - 1

    faces_in[...] = jnp.zeros_like(faces_in)

    barrier = pltpu.get_barrier_semaphore()

    def greet(offset, carry):
        pl.semaphore_signal(
            barrier, inc=1, device_id=(row_peer(me, offset), level), device_id_type=MESH
        )
        return carry

    lax.fori_loop(1, WIDE, greet, 0)

    @pl.when(below)
    def _():
        pl.semaphore_signal(barrier, inc=1, device_id=(me, level - 1), device_id_type=MESH)

    @pl.when(above)
    def _():
        pl.semaphore_signal(barrier, inc=1, device_id=(me, level + 1), device_id_type=MESH)

    pl.semaphore_wait(
        barrier, WIDE - 1 + below.astype(jnp.int32) + above.astype(jnp.int32)
    )

    def label_copy(target, origin):
        return pltpu.make_async_remote_copy(
            src_ref=labels,
            dst_ref=all_labels.at[pl.ds(origin * SLOTS, SLOTS), :],
            send_sem=label_send.at[target],
            recv_sem=label_recv.at[origin],
            device_id=(target, level),
            device_id_type=MESH,
        )

    def send_label(offset, carry):
        label_copy(row_peer(me, offset), me).start()
        return carry

    def slots_of(stage, part):
        rows = pl.ds(part * CHUNK, CHUNK)
        if stage == 0:
            return kappa.at[rows, :]
        return (source if stage % 2 == 0 else fields).at[(stage - 1) // 2, rows, :]

    def spread_copy(stage, target, origin):
        return pltpu.make_async_remote_copy(
            src_ref=slots_of(stage, target),
            dst_ref=received[stage].at[pl.ds(origin * CHUNK, CHUNK), :],
            send_sem=spread_send.at[stage, target],
            recv_sem=spread_recv.at[stage, origin],
            device_id=(target, level),
            device_id_type=MESH,
        )

    def own_spread_copy(stage):
        return pltpu.make_async_copy(
            slots_of(stage, me),
            received[stage].at[pl.ds(me * CHUNK, CHUNK), :],
            own_spread.at[stage],
        )

    def spread(stage, first, last):
        def send_spread(turn, carry):
            spread_copy(stage, row_peer(me, (turn * 7) % WIDE), me).start()
            return carry

        lax.fori_loop(first, last, send_spread, 0)
        if first == 1:
            own_spread_copy(stage).start()

    def place_of(stage, origin):
        if stage == 0:
            return weight.at[pl.ds(origin * PIECE, PIECE), :]
        if stage % 2 == 0:
            return rhs[(stage - 1) // 2].at[pl.ds(origin * PIECE, PIECE), :]
        return cells[(stage - 1) // 2].at[pl.ds(origin * PIECE + PS, PIECE), :]

    def give_copy(stage, target, origin):
        return pltpu.make_async_remote_copy(
            src_ref=sending[stage].at[pl.ds(target * PIECE, PIECE), :],
            dst_ref=place_of(stage, origin),
            send_sem=give_send.at[stage, target],
            recv_sem=give_recv.at[stage, origin],
            device_id=(target, level),
            device_id_type=MESH,
        )

    def own_give_copy(stage):
        return pltpu.make_async_copy(
            sending[stage].at[pl.ds(me * PIECE, PIECE), :],
            place_of(stage, me),
            own_give.at[stage],
        )

    lane = lax.broadcasted_iota(jnp.int32, (8, LANES), 1)
    low_half = lane < 64
    low_quarter = lane % 64 < 32

    def give(stage):
        def wait_spread(turn, carry):
            origin = row_peer(me, turn)
            spread_copy(stage, origin, origin).wait_recv()
            return carry

        lax.fori_loop(1, WIDE, wait_spread, 0)
        own_spread_copy(stage).wait()

        def pick(owner, carry):
            starts = [start_smem[0, owner * 4 + part] for part in range(4)]
            v = [
                [
                    received[stage][pl.ds(start + plane * 64, 8, stride=8), :]
                    for start in starts
                ]
                for plane in range(2)
            ]
            for plane in range(2):
                a, b, c, d = v[plane]
                u = [
                    jnp.where(low_half, a, pltpu.roll(c, 64, 1)),
                    jnp.where(low_half, b, pltpu.roll(d, 64, 1)),
                    jnp.where(low_half, pltpu.roll(a, 64, 1), c),
                    jnp.where(low_half, pltpu.roll(b, 64, 1), d),
                ]
                w = [
                    jnp.where(low_quarter, u[0], pltpu.roll(u[1], 32, 1)),
                    jnp.where(low_quarter, pltpu.roll(u[0], 96, 1), u[1]),
                    jnp.where(low_quarter, u[2], pltpu.roll(u[3], 32, 1)),
                    jnp.where(low_quarter, pltpu.roll(u[2], 96, 1), u[3]),
                ]
                for part in range(4):
                    row = owner * PIECE + plane * PS + part
                    sending[stage][pl.ds(row, 8, stride=4), :] = w[part]
            return carry

        lax.fori_loop(0, WIDE, pick, 0)

        def send_give(turn, carry):
            give_copy(stage, row_peer(me, (turn * 7) % WIDE), me).start()
            return carry

        lax.fori_loop(1, WIDE, send_give, 0)
        own_give_copy(stage).start()

    def wait_given(stage):
        def wait_give(turn, carry):
            origin = row_peer(me, turn)
            give_copy(stage, origin, origin).wait_recv()
            return carry

        lax.fori_loop(1, WIDE, wait_give, 0)
        own_give_copy(stage).wait()

    ways = (
        (above, (me, level + 1), below),
        (below, (me, level - 1), above),
        (right, (me + 1, level), left),
        (left, (me - 1, level), right),
    )

    def face_copy(field, slot, way):
        return pltpu.make_async_remote_copy(
            src_ref=faces_out.at[field, slot, way],
            dst_ref=faces_in.at[field, slot, way],
            send_sem=face_send.at[field, slot, way],
            recv_sem=face_recv.at[field, slot, way],
            device_id=ways[way][1],
            device_id_type=MESH,
        )

    def face_sent(field, step):
        for way in range(4):

            @pl.when(ways[way][0])
            def _():
                face_copy(field, step % 2, way).wait_send()

    def post(field, step):
        slot = step % 2
        if step >= 2:
            face_sent(field, step - 2)
        block = cells[field]
        faces_out[field, slot, 0] = block[PS * PS : (PS + 1) * PS, :]
        faces_out[field, slot, 1] = block[PS : 2 * PS, :]
        for group in range(PS // 8):
            rows, row = pl.ds(group * 8, 8), (group * 8 + 1) * PS
            faces_out[field, slot, 2, rows, :] = block[pl.ds(row + PS - 1, 8, stride=PS), :]
            faces_out[field, slot, 3, rows, :] = block[pl.ds(row, 8, stride=PS), :]
        for way in (2, 3, 0, 1):

            @pl.when(ways[way][0])
            def _():
                face_copy(field, slot, way).start()

    row32 = lax.broadcasted_iota(jnp.int32, (PS, LANES), 0)
    lane32 = lax.broadcasted_iota(jnp.int32, (PS, LANES), 1)
    even = (row32 + lane32) % 2 == 0
    odd = (row32 + lane32) % 2 == 1
    first_row, last_row = row32 == 0, row32 == PS - 1
    first_lane, last_lane = lane32 == 0, lane32 == LANES - 1

    def relax(field, step):
        slot, colour = step % 2, step % 2
        for way in range(4):

            @pl.when(ways[way][2])
            def _():
                face_copy(field, slot, way).wait_recv()

        block, right_side = cells[field], rhs[field]
        block[0:PS, :] = faces_in[field, slot, 0]
        block[(PS + 1) * PS : (PS + 2) * PS, :] = faces_in[field, slot, 1]

        def several(group, carry):
            plane = group * GROUP
            v = [
                block[pl.ds(pl.multiple_of((plane + i) * PS, PS), PS), :]
                for i in range(GROUP + 2)
            ]
            fresh = []
            for i in range(GROUP):
                rows = pl.ds(pl.multiple_of((plane + i) * PS, PS), PS)
                mine = v[i + 1]
                low = jnp.broadcast_to(
                    faces_in[field, slot, 2, pl.ds(plane + i, 1), :], (PS, LANES)
                )
                high = jnp.broadcast_to(
                    faces_in[field, slot, 3, pl.ds(plane + i, 1), :], (PS, LANES)
                )
                total = v[i] + v[i + 2]
                total += jnp.where(first_row, low, pltpu.roll(mine, 1, 0))
                total += jnp.where(last_row, high, pltpu.roll(mine, PS - 1, 0))
                total += jnp.where(first_lane, 0.0, pltpu.roll(mine, 1, 1))
                total += jnp.where(last_lane, 0.0, pltpu.roll(mine, LANES - 1, 1))
                value = (right_side[rows, :] + total) * weight[rows, :] - 0.5 * mine
                fresh.append(jnp.where(even if i % 2 == colour else odd, value, mine))
            for i in range(GROUP):
                if step == HALF_SWEEPS - 1:
                    out[field, plane + i] = fresh[i]
                else:
                    rows = pl.ds(pl.multiple_of((plane + i + 1) * PS, PS), PS)
                    block[rows, :] = fresh[i]
            return carry

        lax.fori_loop(0, PS // GROUP, several, 0)

    lax.fori_loop(1, WIDE, send_label, 0)
    all_labels[pl.ds(me * SLOTS, SLOTS), :] = labels[...]
    for stage in range(STAGES):
        spread(stage, 1, WIDE)

    def wait_label(offset, carry):
        origin = row_peer(me, offset)
        label_copy(origin, origin).wait_recv()
        return carry

    lax.fori_loop(1, WIDE, wait_label, 0)
    slot_row = lax.broadcasted_iota(jnp.int32, (WIDE * SLOTS, LANES), 0)
    wanted = lax.broadcasted_iota(jnp.int32, (WIDE * SLOTS, LANES), 1) + level * (WIDE * 4)
    first = (slot_row // SLOTS) * CHUNK + slot_row % SLOTS
    found = jnp.where(all_labels[...] == wanted, first, 0)
    start_vmem[...] = jnp.max(found, axis=0, keepdims=True)
    move = pltpu.make_async_copy(start_vmem, start_smem, start_sem)
    move.start()
    move.wait()

    for stage in range(STAGES):
        give(stage)
    wait_given(0)

    def invert(block, carry):
        rows = pl.ds(pl.multiple_of(block * PS, PS), PS)
        weight[rows, :] = 1.5 * (1.0 / (6.0 + weight[rows, :]))
        return carry

    lax.fori_loop(0, PS, invert, 0)
    for field in range(3):
        wait_given(2 * field + 1)
        wait_given(2 * field + 2)
        post(field, 0)

    for step in range(HALF_SWEEPS):
        for field in range(3):
            relax(field, step)
            if step < HALF_SWEEPS - 1:
                post(field, step + 1)

    for field in range(3):
        face_sent(field, HALF_SWEEPS - 2)
        face_sent(field, HALF_SWEEPS - 1)

    def drain(offset, carry):
        target = row_peer(me, offset)
        label_copy(target, me).wait_send()
        for stage in range(STAGES):
            spread_copy(stage, target, me).wait_send()
            give_copy(stage, target, me).wait_send()
        return carry

    lax.fori_loop(1, WIDE, drain, 0)


def local(old_fields, old_source, old_kappa, patch_ids):
    def tiles(array):
        lead = array.shape[:-2]
        split = array.reshape(lead + (SLOTS, -1, LANES))
        return jnp.swapaxes(split, -3, -2).reshape(lead + (-1, LANES))

    fields = tiles(jnp.swapaxes(old_fields, 0, 1))
    source = tiles(jnp.swapaxes(old_source, 0, 1))
    kappa = tiles(old_kappa)
    labels = jnp.broadcast_to(patch_ids[:, None], (SLOTS, LANES))
    vmem = pl.BlockSpec(memory_space=pltpu.VMEM)
    anywhere = pl.BlockSpec(memory_space=pl.ANY)
    dma = pltpu.SemaphoreType.DMA
    scratch = (
        [pltpu.VMEM((WIDE * CHUNK, LANES), F32)] * STAGES
        + [pltpu.VMEM((WIDE * PIECE, LANES), F32)] * STAGES
        + [pltpu.VMEM(((PS + 2) * PS, LANES), F32)] * 3
        + [pltpu.VMEM((PS * PS, LANES), F32)] * 3
        + [
            pltpu.VMEM((PS * PS, LANES), F32),
            pltpu.VMEM((WIDE * SLOTS, LANES), jnp.int32),
            pltpu.VMEM((1, LANES), jnp.int32),
            pltpu.SMEM((1, LANES), jnp.int32),
            pltpu.VMEM((3, 2, 4, PS, LANES), F32),
            pltpu.VMEM((3, 2, 4, PS, LANES), F32),
            dma((WIDE,)),
            dma((WIDE,)),
            dma((STAGES, WIDE)),
            dma((STAGES, WIDE)),
            dma((STAGES, WIDE)),
            dma((STAGES, WIDE)),
            dma((STAGES,)),
            dma((STAGES,)),
            dma(()),
            dma((3, 2, 4)),
            dma((3, 2, 4)),
        ]
    )
    return pl.pallas_call(
        kernel,
        out_shape=jax.ShapeDtypeStruct((3, PS, PS, LANES), F32),
        in_specs=[anywhere, anywhere, anywhere, vmem],
        out_specs=vmem,
        scratch_shapes=scratch,
        compiler_params=pltpu.CompilerParams(
            collective_id=0, has_side_effects=True, vmem_limit_bytes=60 << 20
        ),
        name="regrid_and_sweep",
    )(fields, source, kappa, labels)


def solution(mesh):
    in_specs = (
        P(("wide", "narrow"), None, None),
        P(("wide", "narrow"), None, None),
        P(("wide", "narrow"), None),
        P(("wide", "narrow")),
    )
    out_specs = P(None, "narrow", "wide", None)
    return jax.shard_map(local, mesh=mesh, in_specs=in_specs, out_specs=out_specs, check_vma=False)
```

```python
import jax
import jax.numpy as jnp
from jax import lax
from jax.experimental import pallas as pl
from jax.experimental.pallas import tpu as pltpu
from jax.sharding import PartitionSpec as P

PS = 32
SLOTS = 8
LANES = 128
WIDE = 16
STAGES = 7
PLANE = 64
ZONE_IN, DEEP_IN = 96, 32
ZONE_OUT, DEEP_OUT = 48, 16
HALF_SWEEPS = 6
GROUP = 4
MESH = pl.DeviceIdType.MESH
F32 = jnp.float32


def row_peer(me, offset):
    row = lax.rem(me // 4 + offset // 4, 4)
    column = lax.rem(lax.rem(me, 4) + lax.rem(offset, 4), 4)
    return row * 4 + column


def kernel(fields, source, kappa, labels, out, *scratch):
    received, sending, landed = (
        [scratch[group * STAGES : (group + 1) * STAGES] for group in (first, first + 1)]
        for first in (0, 2, 4)
    )
    cells = scratch[6 * STAGES : 6 * STAGES + 3]
    rhs = scratch[6 * STAGES + 3 : 6 * STAGES + 6]
    (
        weight, all_labels, start_vmem, start_smem, faces_out, faces_in,
        label_send, label_recv, spread_send, spread_recv, give_send, give_recv,
        own_spread, own_give, start_sem, face_send, face_recv,
    ) = scratch[6 * STAGES + 6 :]
    me = lax.axis_index("wide")
    level = lax.axis_index("narrow")
    levels = lax.axis_size("narrow")
    below, above = level > 0, level < levels - 1
    left, right = me > 0, me < WIDE - 1

    faces_in[...] = jnp.zeros_like(faces_in)

    barrier = pltpu.get_barrier_semaphore()

    def greet(offset, carry):
        pl.semaphore_signal(
            barrier, inc=1, device_id=(row_peer(me, offset), level), device_id_type=MESH
        )
        return carry

    lax.fori_loop(1, WIDE, greet, 0)

    @pl.when(below)
    def _():
        pl.semaphore_signal(barrier, inc=1, device_id=(me, level - 1), device_id_type=MESH)

    @pl.when(above)
    def _():
        pl.semaphore_signal(barrier, inc=1, device_id=(me, level + 1), device_id_type=MESH)

    pl.semaphore_wait(
        barrier, WIDE - 1 + below.astype(jnp.int32) + above.astype(jnp.int32)
    )

    def label_copy(target, origin):
        return pltpu.make_async_remote_copy(
            src_ref=labels,
            dst_ref=all_labels.at[pl.ds(origin * SLOTS, SLOTS), :],
            send_sem=label_send.at[target],
            recv_sem=label_recv.at[origin],
            device_id=(target, level),
            device_id_type=MESH,
        )

    def send_label(offset, carry):
        label_copy(row_peer(me, offset), me).start()
        return carry

    def outer_plane(part):
        return part + part // 8 * 16

    def pieces(deep):
        return (3,) if deep else (0, 1, 2)

    def slots_of(stage, part, piece):
        inner = (part + 8) * PLANE
        first, count = (
            (outer_plane(part) * PLANE, PLANE), (inner, 16), (inner + 48, 16), (inner + 16, 32),
        )[piece]
        rows = pl.ds(first, count)
        if stage == 0:
            return kappa.at[rows, :]
        return (source if stage % 2 == 0 else fields).at[(stage - 1) // 2, rows, :]

    def slots_at(stage, origin, piece):
        if piece == 3:
            return received[1][stage].at[pl.ds(origin * DEEP_IN, DEEP_IN), :]
        first, count = ((0, PLANE), (PLANE, 16), (PLANE + 16, 16))[piece]
        return received[0][stage].at[pl.ds(origin * ZONE_IN + first, count), :]

    def spread_copy(stage, target, origin, piece):
        return pltpu.make_async_remote_copy(
            src_ref=slots_of(stage, target, piece),
            dst_ref=slots_at(stage, origin, piece),
            send_sem=spread_send.at[stage * 4 + piece, target],
            recv_sem=spread_recv.at[stage * 4 + piece, origin],
            device_id=(target, level),
            device_id_type=MESH,
        )

    def own_spread_copy(stage, piece):
        return pltpu.make_async_copy(
            slots_of(stage, me, piece),
            slots_at(stage, me, piece),
            own_spread.at[stage * 4 + piece],
        )

    def spread(stage, deep):
        def send_spread(turn, carry):
            for piece in pieces(deep):
                spread_copy(stage, row_peer(me, (turn * 7) % WIDE), me, piece).start()
            return carry

        lax.fori_loop(1, WIDE, send_spread, 0)
        for piece in pieces(deep):
            own_spread_copy(stage, piece).start()

    def give_copy(stage, target, origin, deep):
        rows = DEEP_OUT if deep else ZONE_OUT
        return pltpu.make_async_remote_copy(
            src_ref=sending[deep][stage].at[pl.ds(target * rows, rows), :],
            dst_ref=landed[deep][stage].at[pl.ds(origin * rows, rows), :],
            send_sem=give_send.at[stage * 2 + deep, target],
            recv_sem=give_recv.at[stage * 2 + deep, origin],
            device_id=(target, level),
            device_id_type=MESH,
        )

    def own_give_copy(stage, deep):
        rows = pl.ds(me * (DEEP_OUT if deep else ZONE_OUT), DEEP_OUT if deep else ZONE_OUT)
        return pltpu.make_async_copy(
            sending[deep][stage].at[rows, :],
            landed[deep][stage].at[rows, :],
            own_give.at[stage * 2 + deep],
        )

    def turn_over(patches, lines):
        lane = lax.broadcasted_iota(jnp.int32, (lines, LANES), 1)
        low_half = lane < 64
        low_quarter = lane % 64 < 32
        a, b, c, d = patches
        u = [
            jnp.where(low_half, a, pltpu.roll(c, 64, 1)),
            jnp.where(low_half, b, pltpu.roll(d, 64, 1)),
            jnp.where(low_half, pltpu.roll(a, 64, 1), c),
            jnp.where(low_half, pltpu.roll(b, 64, 1), d),
        ]
        return [
            jnp.where(low_quarter, u[0], pltpu.roll(u[1], 32, 1)),
            jnp.where(low_quarter, pltpu.roll(u[0], 96, 1), u[1]),
            jnp.where(low_quarter, u[2], pltpu.roll(u[3], 32, 1)),
            jnp.where(low_quarter, pltpu.roll(u[2], 96, 1), u[3]),
        ]

    def give(stage, deep):
        def wait_spread(turn, carry):
            origin = row_peer(me, turn)
            for piece in pieces(deep):
                spread_copy(stage, origin, origin, piece).wait_recv()
            return carry

        lax.fori_loop(1, WIDE, wait_spread, 0)
        for piece in pieces(deep):
            own_spread_copy(stage, piece).wait()
        source_rows, finished = received[deep][stage], sending[deep][stage]
        runs = ((0, 4, 0),) if deep else ((0, 8, 0), (PLANE, 4, 32))

        def pick(owner, carry):
            starts = [start_smem[deep, owner * 4 + part] for part in range(4)]
            taken = [
                [source_rows[pl.ds(start + first, lines, stride=8), :] for start in starts]
                for first, lines, _ in runs
            ]
            for (_, lines, row), patches in zip(runs, taken):
                base = owner * (DEEP_OUT if deep else ZONE_OUT) + row
                for part, value in enumerate(turn_over(patches, lines)):
                    finished[pl.ds(base + part, lines, stride=4), :] = value
            return carry

        lax.fori_loop(0, WIDE, pick, 0)

        def send_give(turn, carry):
            give_copy(stage, row_peer(me, (turn * 7) % WIDE), me, deep).start()
            return carry

        lax.fori_loop(1, WIDE, send_give, 0)
        own_give_copy(stage, deep).start()

    def settle(stage, deep):
        def wait_give(turn, carry):
            origin = row_peer(me, turn)
            give_copy(stage, origin, origin, deep).wait_recv()
            return carry

        lax.fori_loop(1, WIDE, wait_give, 0)
        own_give_copy(stage, deep).wait()
        shift = 0
        if stage == 0:
            home = weight
        elif stage % 2 == 0:
            home = rhs[(stage - 1) // 2]
        else:
            home, shift = cells[(stage - 1) // 2], 1
        here = landed[deep][stage]

        def put(part, carry):
            outer = (outer_plane(part) + shift) * PS
            inner = (part + 8 + shift) * PS
            moves = (
                ((0, inner + 8, 16),)
                if deep
                else ((0, outer, 32), (32, inner, 8), (40, inner + 24, 8))
            )
            for first, row, count in moves:
                first += part * (DEEP_OUT if deep else ZONE_OUT)
                value = here[pl.ds(pl.multiple_of(first, 8), count), :]
                if stage == 0:
                    value = 1.5 * (1.0 / (6.0 + value))
                home[pl.ds(pl.multiple_of(row, 8), count), :] = value
            return carry

        lax.fori_loop(0, WIDE, put, 0)

    ways = (
        (above, (me, level + 1), below),
        (below, (me, level - 1), above),
        (right, (me + 1, level), left),
        (left, (me - 1, level), right),
    )

    def face_copy(field, slot, way):
        return pltpu.make_async_remote_copy(
            src_ref=faces_out.at[field, slot, way],
            dst_ref=faces_in.at[field, slot, way],
            send_sem=face_send.at[field, slot, way],
            recv_sem=face_recv.at[field, slot, way],
            device_id=ways[way][1],
            device_id_type=MESH,
        )

    def face_sent(field, step):
        for way in range(4):

            @pl.when(ways[way][0])
            def _():
                face_copy(field, step % 2, way).wait_send()

    def post(field, step):
        slot = step % 2
        if step >= 2:
            face_sent(field, step - 2)
        block = cells[field]
        faces_out[field, slot, 0] = block[PS * PS : (PS + 1) * PS, :]
        faces_out[field, slot, 1] = block[PS : 2 * PS, :]
        for group in range(PS // 8):
            rows, row = pl.ds(group * 8, 8), (group * 8 + 1) * PS
            faces_out[field, slot, 2, rows, :] = block[pl.ds(row + PS - 1, 8, stride=PS), :]
            faces_out[field, slot, 3, rows, :] = block[pl.ds(row, 8, stride=PS), :]
        for way in (2, 3, 0, 1):

            @pl.when(ways[way][0])
            def _():
                face_copy(field, slot, way).start()

    def new_values(v, low, high, right_side, w, chosen):
        rows = v[0].shape[0]
        row = lax.broadcasted_iota(jnp.int32, (rows, LANES), 0)
        lane = lax.broadcasted_iota(jnp.int32, (rows, LANES), 1)
        fresh = []
        for i in range(len(v) - 2):
            mine = v[i + 1]
            back, forth = pltpu.roll(mine, 1, 0), pltpu.roll(mine, rows - 1, 0)
            if low is not None:
                back = jnp.where(row == 0, jnp.broadcast_to(low[i], mine.shape), back)
            if high is not None:
                forth = jnp.where(row == rows - 1, jnp.broadcast_to(high[i], mine.shape), forth)
            total = v[i] + v[i + 2] + back + forth
            total += jnp.where(lane == 0, 0.0, pltpu.roll(mine, 1, 1))
            total += jnp.where(lane == LANES - 1, 0.0, pltpu.roll(mine, LANES - 1, 1))
            value = (right_side[i] + total) * w[i] - 0.5 * mine
            fresh.append(jnp.where(chosen[i], value, mine))
        return fresh

    row32 = lax.broadcasted_iota(jnp.int32, (PS, LANES), 0)
    lane32 = lax.broadcasted_iota(jnp.int32, (PS, LANES), 1)
    row_reach = jnp.abs(2 * row32 - (PS - 1))
    even = (row32 + lane32) % 2 == 0
    odd = (row32 + lane32) % 2 == 1

    def relax_outside(field, step):
        slot, colour = step % 2, step % 2
        for way in range(4):

            @pl.when(ways[way][2])
            def _():
                face_copy(field, slot, way).wait_recv()

        block, right_side = cells[field], rhs[field]
        block[0:PS, :] = faces_in[field, slot, 0]
        block[(PS + 1) * PS : (PS + 2) * PS, :] = faces_in[field, slot, 1]

        def part_of(array, plane, first, count):
            return array[pl.ds(pl.multiple_of(plane * PS + first, 8), count), :]

        def several(group, carry):
            plane = group * GROUP + group // 2 * 16
            fresh = new_values(
                [part_of(block, plane + i, 0, PS) for i in range(GROUP + 2)],
                [faces_in[field, slot, 2, pl.ds(plane + i, 1), :] for i in range(GROUP)],
                [faces_in[field, slot, 3, pl.ds(plane + i, 1), :] for i in range(GROUP)],
                [part_of(right_side, plane + i, 0, PS) for i in range(GROUP)],
                [part_of(weight, plane + i, 0, PS) for i in range(GROUP)],
                [
                    (even if i % 2 == colour else odd)
                    & (
                        jnp.maximum(row_reach, jnp.abs(2 * (plane + i) - (PS - 1)))
                        >= 19 + 2 * step
                    )
                    for i in range(GROUP)
                ],
            )
            for i in range(GROUP):
                rows = pl.ds(pl.multiple_of((plane + i + 1) * PS, PS), PS)
                block[rows, :] = fresh[i]
            return carry

        lax.fori_loop(0, 4, several, 0)
        row8 = lax.broadcasted_iota(jnp.int32, (8, LANES), 0)
        lane8 = lax.broadcasted_iota(jnp.int32, (8, LANES), 1)
        reach = (row8 <= 6 - step, row8 >= 1 + step)

        def ends(group, carry):
            plane = group * GROUP + 8
            fresh = []
            for end, first in ((0, 0), (1, 24)):
                line = [
                    faces_in[field, slot, 2 + end, pl.ds(plane + i, 1), :] for i in range(GROUP)
                ]
                fresh.append(
                    new_values(
                        [part_of(block, plane + i, first, 8) for i in range(GROUP + 2)],
                        line if end == 0 else None,
                        line if end == 1 else None,
                        [part_of(right_side, plane + i, first, 8) for i in range(GROUP)],
                        [part_of(weight, plane + i, first, 8) for i in range(GROUP)],
                        [
                            ((row8 + lane8 + i) % 2 == colour) & reach[end]
                            for i in range(GROUP)
                        ],
                    )
                )
            for end, first in ((0, 0), (1, 24)):
                for i in range(GROUP):
                    row = (plane + i + 1) * PS + first
                    block[pl.ds(pl.multiple_of(row, 8), 8), :] = fresh[end][i]
            return carry

        lax.fori_loop(0, 4, ends, 0)

    def relax_inside(field, step):
        colour = step % 2
        block, right_side = cells[field], rhs[field]
        start, groups = ((6, 5), (6, 5), (4, 6), (4, 6), (2, 7), (0, 8))[step]

        def several(group, carry):
            plane = group * GROUP + start

            def whole(array, i):
                return array[pl.ds(pl.multiple_of((plane + i) * PS, PS), PS), :]

            fresh = new_values(
                [whole(block, i) for i in range(GROUP + 2)],
                None,
                None,
                [whole(right_side, i) for i in range(GROUP)],
                [whole(weight, i) for i in range(GROUP)],
                [
                    (even if i % 2 == colour else odd)
                    & (
                        jnp.maximum(row_reach, jnp.abs(2 * (plane + i) - (PS - 1)))
                        < 19 + 2 * step
                    )
                    for i in range(GROUP)
                ],
            )
            for i in range(GROUP):
                if step == HALF_SWEEPS - 1:
                    out[field, plane + i] = fresh[i]
                else:
                    rows = pl.ds(pl.multiple_of((plane + i + 1) * PS, PS), PS)
                    block[rows, :] = fresh[i]
            return carry

        lax.fori_loop(0, groups, several, 0)

    lax.fori_loop(1, WIDE, send_label, 0)
    all_labels[pl.ds(me * SLOTS, SLOTS), :] = labels[...]
    for stage in range(STAGES):
        spread(stage, 0)

    def wait_label(offset, carry):
        origin = row_peer(me, offset)
        label_copy(origin, origin).wait_recv()
        return carry

    lax.fori_loop(1, WIDE, wait_label, 0)
    slot_row = lax.broadcasted_iota(jnp.int32, (WIDE * SLOTS, LANES), 0)
    wanted = lax.broadcasted_iota(jnp.int32, (WIDE * SLOTS, LANES), 1) + level * (WIDE * 4)
    for deep, rows in ((0, ZONE_IN), (1, DEEP_IN)):
        first = (slot_row // SLOTS) * rows + slot_row % SLOTS
        found = jnp.where(all_labels[...] == wanted, first, 0)
        start_vmem[deep : deep + 1, :] = jnp.max(found, axis=0, keepdims=True)
    move = pltpu.make_async_copy(start_vmem, start_smem, start_sem)
    move.start()
    move.wait()

    for stage in range(STAGES):
        give(stage, 0)
    for stage in range(2):
        spread(stage, 1)
    settle(0, 0)
    for field in range(3):
        settle(2 * field + 1, 0)
        settle(2 * field + 2, 0)
        post(field, 0)

    between = (
        ((spread, 2), (spread, 3)),
        ((give, 0), (spread, 4)),
        ((give, 1), (give, 2), (spread, 5)),
        ((give, 3), (spread, 6)),
        ((give, 4), (give, 5)),
        ((give, 6),),
    )
    for step in range(HALF_SWEEPS):
        for move_on, stage in between[step]:
            move_on(stage, 1)
        for field in range(3):
            relax_outside(field, step)
            if step < HALF_SWEEPS - 1:
                post(field, step + 1)
    settle(0, 1)
    for field in range(3):
        settle(2 * field + 1, 1)
        settle(2 * field + 2, 1)
        for step in range(HALF_SWEEPS):
            relax_inside(field, step)

    for field in range(3):
        face_sent(field, HALF_SWEEPS - 2)
        face_sent(field, HALF_SWEEPS - 1)

    def drain(offset, carry):
        target = row_peer(me, offset)
        label_copy(target, me).wait_send()
        for stage in range(STAGES):
            for piece in range(4):
                spread_copy(stage, target, me, piece).wait_send()
            for deep in range(2):
                give_copy(stage, target, me, deep).wait_send()
        return carry

    lax.fori_loop(1, WIDE, drain, 0)


def local(old_fields, old_source, old_kappa, patch_ids):
    def tiles(array):
        lead = array.shape[:-2]
        split = array.reshape(lead + (SLOTS, -1, LANES))
        return jnp.swapaxes(split, -3, -2).reshape(lead + (-1, LANES))

    fields = tiles(jnp.swapaxes(old_fields, 0, 1))
    source = tiles(jnp.swapaxes(old_source, 0, 1))
    kappa = tiles(old_kappa)
    labels = jnp.broadcast_to(patch_ids[:, None], (SLOTS, LANES))
    vmem = pl.BlockSpec(memory_space=pltpu.VMEM)
    anywhere = pl.BlockSpec(memory_space=pl.ANY)
    dma = pltpu.SemaphoreType.DMA
    scratch = (
        [
            pltpu.VMEM((WIDE * rows, LANES), F32)
            for rows in (ZONE_IN, DEEP_IN, ZONE_OUT, DEEP_OUT, ZONE_OUT, DEEP_OUT)
            for _ in range(STAGES)
        ]
        + [pltpu.VMEM(((PS + 2) * PS, LANES), F32)] * 3
        + [pltpu.VMEM((PS * PS, LANES), F32)] * 3
        + [
            pltpu.VMEM((PS * PS, LANES), F32),
            pltpu.VMEM((WIDE * SLOTS, LANES), jnp.int32),
            pltpu.VMEM((2, LANES), jnp.int32),
            pltpu.SMEM((2, LANES), jnp.int32),
            pltpu.VMEM((3, 2, 4, PS, LANES), F32),
            pltpu.VMEM((3, 2, 4, PS, LANES), F32),
            dma((WIDE,)),
            dma((WIDE,)),
            dma((STAGES * 4, WIDE)),
            dma((STAGES * 4, WIDE)),
            dma((STAGES * 2, WIDE)),
            dma((STAGES * 2, WIDE)),
            dma((STAGES * 4,)),
            dma((STAGES * 2,)),
            dma(()),
            dma((3, 2, 4)),
            dma((3, 2, 4)),
        ]
    )
    return pl.pallas_call(
        kernel,
        out_shape=jax.ShapeDtypeStruct((3, PS, PS, LANES), F32),
        in_specs=[anywhere, anywhere, anywhere, vmem],
        out_specs=vmem,
        scratch_shapes=scratch,
        compiler_params=pltpu.CompilerParams(
            collective_id=0, has_side_effects=True, vmem_limit_bytes=60 << 20
        ),
        name="regrid_and_sweep",
    )(fields, source, kappa, labels)


def solution(mesh):
    in_specs = (
        P(("wide", "narrow"), None, None),
        P(("wide", "narrow"), None, None),
        P(("wide", "narrow"), None),
        P(("wide", "narrow")),
    )
    out_specs = P(None, "narrow", "wide", None)
    return jax.shard_map(local, mesh=mesh, in_specs=in_specs, out_specs=out_specs, check_vma=False)
```

```python
import jax
import jax.numpy as jnp
from jax import lax
from jax.experimental import pallas as pl
from jax.experimental.pallas import tpu as pltpu
from jax.sharding import PartitionSpec as P

PS = 32
SLOTS = 8
LANES = 128
WIDE = 16
STAGES = 7
FIELD, SIDE = 1, 4
CHUNK = 128
PIECE = 64
HALF_SWEEPS = 6
GROUP = 4
MESH = pl.DeviceIdType.MESH
F32 = jnp.float32


def row_peer(me, offset):
    row = lax.rem(me // 4 + offset // 4, 4)
    column = lax.rem(lax.rem(me, 4) + lax.rem(offset, 4), 4)
    return row * 4 + column


def kernel(fields, source, kappa, ids, out, *scratch):
    received = scratch[0:STAGES]
    sending = scratch[STAGES : 2 * STAGES]
    cells = scratch[2 * STAGES : 2 * STAGES + 3]
    rhs = scratch[2 * STAGES + 3 : 2 * STAGES + 6]
    (
        labels, weight, lines, all_labels, start_vmem, start_smem, faces_out, faces_in,
        label_send, label_recv, spread_send, spread_recv, give_send, give_recv,
        own_spread, own_give, start_sem, face_send, face_recv,
    ) = scratch[2 * STAGES + 6 :]
    me = lax.axis_index("wide")
    level = lax.axis_index("narrow")
    levels = lax.axis_size("narrow")
    below, above = level > 0, level < levels - 1
    left, right = me > 0, me < WIDE - 1

    tile_row = lax.broadcasted_iota(jnp.int32, (SLOTS, LANES), 0)
    tile = jnp.zeros((SLOTS, LANES), jnp.int32)
    for entry in range(SLOTS):
        tile = jnp.where(tile_row == entry, ids[entry], tile)
    labels[...] = tile

    faces_in[...] = jnp.zeros_like(faces_in)

    barrier = pltpu.get_barrier_semaphore()

    def greet(offset, carry):
        pl.semaphore_signal(
            barrier, inc=1, device_id=(row_peer(me, offset), level), device_id_type=MESH
        )
        return carry

    lax.fori_loop(1, WIDE, greet, 0)

    @pl.when(below)
    def _():
        pl.semaphore_signal(barrier, inc=1, device_id=(me, level - 1), device_id_type=MESH)

    @pl.when(above)
    def _():
        pl.semaphore_signal(barrier, inc=1, device_id=(me, level + 1), device_id_type=MESH)

    pl.semaphore_wait(
        barrier, WIDE - 1 + below.astype(jnp.int32) + above.astype(jnp.int32)
    )

    def label_copy(target, origin):
        return pltpu.make_async_remote_copy(
            src_ref=labels,
            dst_ref=all_labels.at[pl.ds(origin * SLOTS, SLOTS), :],
            send_sem=label_send.at[target],
            recv_sem=label_recv.at[origin],
            device_id=(target, level),
            device_id_type=MESH,
        )

    def send_label(offset, carry):
        label_copy(row_peer(me, offset), me).start()
        return carry

    def slots_of(stage, part):
        rows = pl.ds(part * CHUNK, CHUNK)
        if stage == 0:
            return kappa.at[rows, :]
        if stage < SIDE:
            return fields.at[stage - FIELD, rows, :]
        return source.at[stage - SIDE, rows, :]

    def spread_copy(stage, target, origin):
        return pltpu.make_async_remote_copy(
            src_ref=slots_of(stage, target),
            dst_ref=received[stage].at[pl.ds(origin * CHUNK, CHUNK), :],
            send_sem=spread_send.at[stage, target],
            recv_sem=spread_recv.at[stage, origin],
            device_id=(target, level),
            device_id_type=MESH,
        )

    def own_spread_copy(stage):
        return pltpu.make_async_copy(
            slots_of(stage, me),
            received[stage].at[pl.ds(me * CHUNK, CHUNK), :],
            own_spread.at[stage],
        )

    def spread(stage, first, last):
        def send_spread(turn, carry):
            spread_copy(stage, row_peer(me, (turn * 7) % WIDE), me).start()
            return carry

        lax.fori_loop(first, last, send_spread, 0)
        if first == 1:
            own_spread_copy(stage).start()

    def place_of(stage, origin):
        if stage == 0:
            return weight.at[pl.ds(origin * PIECE, PIECE), :]
        if stage < SIDE:
            return cells[stage - FIELD].at[pl.ds(origin * PIECE + PS, PIECE), :]
        return rhs[stage - SIDE].at[pl.ds(origin * PIECE, PIECE), :]

    def give_copy(stage, target, origin):
        return pltpu.make_async_remote_copy(
            src_ref=sending[stage].at[pl.ds(target * PIECE, PIECE), :],
            dst_ref=place_of(stage, origin),
            send_sem=give_send.at[stage, target],
            recv_sem=give_recv.at[stage, origin],
            device_id=(target, level),
            device_id_type=MESH,
        )

    def own_give_copy(stage):
        return pltpu.make_async_copy(
            sending[stage].at[pl.ds(me * PIECE, PIECE), :],
            place_of(stage, me),
            own_give.at[stage],
        )

    lane = lax.broadcasted_iota(jnp.int32, (8, LANES), 1)
    low_half = lane < 64
    low_quarter = lane % 64 < 32

    def give(stage):
        def wait_spread(turn, carry):
            origin = row_peer(me, turn)
            spread_copy(stage, origin, origin).wait_recv()
            return carry

        lax.fori_loop(1, WIDE, wait_spread, 0)
        own_spread_copy(stage).wait()

        def pick(owner, carry):
            starts = [start_smem[0, owner * 4 + part] for part in range(4)]
            v = [
                [
                    received[stage][pl.ds(start + plane * 64, 8, stride=8), :]
                    for start in starts
                ]
                for plane in range(2)
            ]
            for plane in range(2):
                a, b, c, d = v[plane]
                u = [
                    jnp.where(low_half, a, pltpu.roll(c, 64, 1)),
                    jnp.where(low_half, b, pltpu.roll(d, 64, 1)),
                    jnp.where(low_half, pltpu.roll(a, 64, 1), c),
                    jnp.where(low_half, pltpu.roll(b, 64, 1), d),
                ]
                w = [
                    jnp.where(low_quarter, u[0], pltpu.roll(u[1], 32, 1)),
                    jnp.where(low_quarter, pltpu.roll(u[0], 96, 1), u[1]),
                    jnp.where(low_quarter, u[2], pltpu.roll(u[3], 32, 1)),
                    jnp.where(low_quarter, pltpu.roll(u[2], 96, 1), u[3]),
                ]
                for part in range(4):
                    row = owner * PIECE + plane * PS + part
                    sending[stage][pl.ds(row, 8, stride=4), :] = w[part]
            return carry

        lax.fori_loop(0, WIDE, pick, 0)

        def send_give(turn, carry):
            give_copy(stage, row_peer(me, (turn * 7) % WIDE), me).start()
            return carry

        lax.fori_loop(1, WIDE, send_give, 0)
        own_give_copy(stage).start()

    def wait_given(stage):
        def wait_give(turn, carry):
            origin = row_peer(me, turn)
            give_copy(stage, origin, origin).wait_recv()
            return carry

        lax.fori_loop(1, WIDE, wait_give, 0)
        own_give_copy(stage).wait()

    ways = (
        (above, (me, level + 1), below),
        (below, (me, level - 1), above),
        (right, (me + 1, level), left),
        (left, (me - 1, level), right),
    )

    def face_copy(field, slot, way):
        return pltpu.make_async_remote_copy(
            src_ref=faces_out.at[field, slot, way],
            dst_ref=faces_in.at[field, slot, way],
            send_sem=face_send.at[field, slot, way],
            recv_sem=face_recv.at[field, slot, way],
            device_id=ways[way][1],
            device_id_type=MESH,
        )

    def face_sent(field, step):
        for way in range(4):

            @pl.when(ways[way][0])
            def _():
                face_copy(field, step % 2, way).wait_send()

    row8 = lax.broadcasted_iota(jnp.int32, (8, LANES), 0)
    lane8 = lax.broadcasted_iota(jnp.int32, (8, LANES), 1)

    def post(field, step):
        slot = step % 2
        if step >= 2:
            face_sent(field, step - 2)
        block = cells[field]
        for way, near in ((2, PS - 1), (3, 0), (0, PS - 1), (1, 0)):
            if way < 2:
                start = (near + 1) * PS
                face = [block[start + 8 * i : start + 8 * i + 8, :] for i in range(4)]
            else:
                face = [block[pl.ds((8 * i + 1) * PS + near, 8, stride=PS), :] for i in range(4)]
            kept = (row8 + lane8) % 2 == (1 - step % 2 + near) % 2
            for i in range(2):
                mixed = jnp.where(kept, face[i], pltpu.roll(face[i + 2], 1, 1))
                faces_out[field, slot, way, 8 * i : 8 * i + 8, :] = mixed
        for way in (2, 3, 0, 1):

            @pl.when(ways[way][0])
            def _():
                face_copy(field, slot, way).start()

    row32 = lax.broadcasted_iota(jnp.int32, (PS, LANES), 0)
    lane32 = lax.broadcasted_iota(jnp.int32, (PS, LANES), 1)
    even = (row32 + lane32) % 2 == 0
    odd = (row32 + lane32) % 2 == 1
    first_row, last_row = row32 == 0, row32 == PS - 1
    first_lane, last_lane = lane32 == 0, lane32 == LANES - 1

    def relax(field, step):
        slot, colour = step % 2, step % 2
        for way in range(4):

            @pl.when(ways[way][2])
            def _():
                face_copy(field, slot, way).wait_recv()

        block, right_side = cells[field], rhs[field]
        for way in range(4):
            home, start = ((block, 0), (block, (PS + 1) * PS), (lines.at[field, 0], 0), (lines.at[field, 1], 0))[way]
            mixed = faces_in[field, slot, way]
            home[start : start + PS // 2, :] = mixed
            home[start + PS // 2 : start + PS, :] = pltpu.roll(mixed, LANES - 1, 1)

        def several(group, carry):
            plane = group * GROUP
            v = [
                block[pl.ds(pl.multiple_of((plane + i) * PS, PS), PS), :]
                for i in range(GROUP + 2)
            ]
            fresh = []
            for i in range(GROUP):
                rows = pl.ds(pl.multiple_of((plane + i) * PS, PS), PS)
                mine = v[i + 1]
                low = jnp.broadcast_to(
                    lines[field, 0, pl.ds(plane + i, 1), :], (PS, LANES)
                )
                high = jnp.broadcast_to(
                    lines[field, 1, pl.ds(plane + i, 1), :], (PS, LANES)
                )
                total = v[i] + v[i + 2]
                total += jnp.where(first_row, low, pltpu.roll(mine, 1, 0))
                total += jnp.where(last_row, high, pltpu.roll(mine, PS - 1, 0))
                total += jnp.where(first_lane, 0.0, pltpu.roll(mine, 1, 1))
                total += jnp.where(last_lane, 0.0, pltpu.roll(mine, LANES - 1, 1))
                value = (right_side[rows, :] + total) * weight[rows, :] - 0.5 * mine
                fresh.append(jnp.where(even if i % 2 == colour else odd, value, mine))
            for i in range(GROUP):
                if step == HALF_SWEEPS - 1:
                    out[field, plane + i] = fresh[i]
                else:
                    rows = pl.ds(pl.multiple_of((plane + i + 1) * PS, PS), PS)
                    block[rows, :] = fresh[i]
            return carry

        lax.fori_loop(0, PS // GROUP, several, 0)

    lax.fori_loop(1, WIDE, send_label, 0)
    all_labels[pl.ds(me * SLOTS, SLOTS), :] = labels[...]
    for stage in range(STAGES):
        spread(stage, 1, WIDE)

    def wait_label(offset, carry):
        origin = row_peer(me, offset)
        label_copy(origin, origin).wait_recv()
        return carry

    lax.fori_loop(1, WIDE, wait_label, 0)
    slot_row = lax.broadcasted_iota(jnp.int32, (WIDE * SLOTS, LANES), 0)
    wanted = lax.broadcasted_iota(jnp.int32, (WIDE * SLOTS, LANES), 1) + level * (WIDE * 4)
    first = (slot_row // SLOTS) * CHUNK + slot_row % SLOTS
    found = jnp.where(all_labels[...] == wanted, first, 0)
    start_vmem[...] = jnp.max(found, axis=0, keepdims=True)
    move = pltpu.make_async_copy(start_vmem, start_smem, start_sem)
    move.start()
    move.wait()

    for stage in range(STAGES):
        give(stage)
    wait_given(0)

    def invert(block, carry):
        rows = pl.ds(pl.multiple_of(block * PS, PS), PS)
        weight[rows, :] = 1.5 * (1.0 / (6.0 + weight[rows, :]))
        return carry

    lax.fori_loop(0, PS, invert, 0)
    for field in range(3):
        wait_given(FIELD + field)
        post(field, 0)

    for step in range(HALF_SWEEPS):
        for field in range(3):
            if step == 0:
                wait_given(SIDE + field)
            relax(field, step)
            if step < HALF_SWEEPS - 1:
                post(field, step + 1)

    for field in range(3):
        face_sent(field, HALF_SWEEPS - 2)
        face_sent(field, HALF_SWEEPS - 1)

    def drain(offset, carry):
        target = row_peer(me, offset)
        label_copy(target, me).wait_send()
        for stage in range(STAGES):
            spread_copy(stage, target, me).wait_send()
            give_copy(stage, target, me).wait_send()
        return carry

    lax.fori_loop(1, WIDE, drain, 0)


def local(old_fields, old_source, old_kappa, patch_ids):
    def tiles(array):
        lead = array.shape[:-2]
        split = array.reshape(lead + (SLOTS, -1, LANES))
        return jnp.swapaxes(split, -3, -2).reshape(lead + (-1, LANES))

    fields = tiles(jnp.swapaxes(old_fields, 0, 1))
    source = tiles(jnp.swapaxes(old_source, 0, 1))
    kappa = tiles(old_kappa)
    vmem = pl.BlockSpec(memory_space=pltpu.VMEM)
    anywhere = pl.BlockSpec(memory_space=pl.ANY)
    dma = pltpu.SemaphoreType.DMA
    scratch = (
        [pltpu.VMEM((WIDE * CHUNK, LANES), F32)] * STAGES
        + [pltpu.VMEM((WIDE * PIECE, LANES), F32)] * STAGES
        + [pltpu.VMEM(((PS + 2) * PS, LANES), F32)] * 3
        + [pltpu.VMEM((PS * PS, LANES), F32)] * 3
        + [
            pltpu.VMEM((SLOTS, LANES), jnp.int32),
            pltpu.VMEM((PS * PS, LANES), F32),
            pltpu.VMEM((3, 2, PS, LANES), F32),
            pltpu.VMEM((WIDE * SLOTS, LANES), jnp.int32),
            pltpu.VMEM((1, LANES), jnp.int32),
            pltpu.SMEM((1, LANES), jnp.int32),
            pltpu.VMEM((3, 2, 4, PS // 2, LANES), F32),
            pltpu.VMEM((3, 2, 4, PS // 2, LANES), F32),
            dma((WIDE,)),
            dma((WIDE,)),
            dma((STAGES, WIDE)),
            dma((STAGES, WIDE)),
            dma((STAGES, WIDE)),
            dma((STAGES, WIDE)),
            dma((STAGES,)),
            dma((STAGES,)),
            dma(()),
            dma((3, 2, 4)),
            dma((3, 2, 4)),
        ]
    )
    return pl.pallas_call(
        kernel,
        out_shape=jax.ShapeDtypeStruct((3, PS, PS, LANES), F32),
        in_specs=[anywhere, anywhere, anywhere, pl.BlockSpec(memory_space=pltpu.SMEM)],
        out_specs=vmem,
        scratch_shapes=scratch,
        compiler_params=pltpu.CompilerParams(
            collective_id=0, has_side_effects=True, vmem_limit_bytes=60 << 20
        ),
        name="regrid_and_sweep",
    )(fields, source, kappa, patch_ids)


def solution(mesh):
    in_specs = (
        P(("wide", "narrow"), None, None),
        P(("wide", "narrow"), None, None),
        P(("wide", "narrow"), None),
        P(("wide", "narrow")),
    )
    out_specs = P(None, "narrow", "wide", None)
    return jax.shard_map(local, mesh=mesh, in_specs=in_specs, out_specs=out_specs, check_vma=False)
```
